256 devices in a mesh: fibre: 32 (over x, y, core), group: 8 (over z).
Axes of the slice: x: 4, y: 4, z: 8, core: 2. Of those that a mesh axis runs over, the one named last changes fastest.
Arguments:
- tensor: float32 [512, 393216], P('fibre', 'group'), as said below
Outputs:
- basis: float32 [512, 393216], P('fibre', 'group')
- factor: float32 [512, 512], replicated
Inputs may be any that keep to these rules, and one draw needn't show every extreme that they name: `tensor`: entries are real-valued and the unfolding has full row rank.
All inputs are finite; a program needn't handle non-finite values.
Results may differ from the reference program's by a relative error of at most 0.00018.
Values sent between devices are 32-bit elements; how exact they have to be, the bound alone decides.
A program may use at most 64 MiB of HBM per device.

```python
import jax
import jax.numpy as jnp
from jax import lax

M = 512
ROWS_DEV = 1536
COLS = 393216
N_FIBRE = 32
N_GROUP = 8


def draw_tensor(key, part):
    keys = jax.random.split(key, 6)
    base = jax.random.normal(keys[0], (M, COLS), jnp.float32)
    loadings = jax.random.normal(keys[4], (M, 8), jnp.float32) / jnp.sqrt(8.0)
    common = jax.random.normal(keys[5], (8, COLS), jnp.float32)
    shared = jnp.zeros((M, COLS), jnp.float32)
    for factor_index in range(8):
        shared = shared + loadings[:, factor_index:factor_index + 1] * common[factor_index:factor_index + 1, :]
    base = base + 0.8 * shared
    row_scale = jnp.exp(jax.random.uniform(keys[1], (M, 1), jnp.float32) * jnp.log(4.0))
    position = jnp.arange(COLS, dtype=jnp.float32).reshape(1, COLS) / COLS
    col_scale = jnp.exp(position * jnp.log(3.0) + jax.random.uniform(keys[2], (1, COLS), jnp.float32, -0.3, 0.3))
    return (base * row_scale * col_scale).astype(jnp.float32)


def setup_inputs(seed: int = 0) -> dict:
    splits = jax.random.split(jax.random.key(seed), 2)
    return {
        "tensor": draw_tensor(jax.random.fold_in(splits[1], 71), 0),
    }


def reference(tensor):
    count_f = N_FIBRE
    count_g = N_GROUP
    total_cols = ROWS_DEV * count_f * count_g
    blocks = tensor.reshape(M, count_g, count_f, ROWS_DEV).transpose(2, 1, 0, 3).reshape(count_f * count_g, M, ROWS_DEV)

    def add_gram(carry, block):
        gram = jnp.dot(block.astype(jnp.float32), block.T.astype(jnp.float32), precision=lax.Precision.HIGHEST, preferred_element_type=jnp.float32) / total_cols
        return (carry + gram, None)
    total, unused = lax.scan(add_gram, jnp.zeros((M, M), jnp.float32), blocks)
    factor = jnp.linalg.cholesky(total)

    def solve_block(block):
        return lax.linalg.triangular_solve(factor, block, left_side=True, lower=True)
    solved = lax.map(solve_block, blocks).reshape(count_f, count_g, M, ROWS_DEV)
    basis = solved.transpose(2, 1, 0, 3).reshape(M, total_cols)
    return (basis, factor)
```

```python
import jax
import jax.numpy as jnp
from jax import lax
from jax.experimental import pallas as pl
from jax.experimental.pallas import tpu as pltpu
from jax.sharding import PartitionSpec as P

HI = lax.Precision.HIGHEST
MESH = pl.DeviceIdType.MESH
M = 512
NF = 32
NG = 8
W = 1536
COLS = W * NF * NG
PACK = 1280
OWN = PACK // NF
FAR = sorted(
    [(dx, dy, dc) for dx in range(4) for dy in range(4) for dc in range(2) if (dx, dy, dc) != (0, 0, 0)],
    key=lambda t: -(min(t[0], 4 - t[0]) + min(t[1], 4 - t[1])),
)


def peer(me, t):
    x, y, c = me // 8, (me // 2) % 4, me % 2
    return ((x + t[0]) % 4 * 4 + (y + t[1]) % 4) * 2 + (c + t[2]) % 2


def rows(i, n):
    return pl.ds(pl.multiple_of(i * n, 8), n)


def lanes(i, n):
    return pl.ds(pl.multiple_of(i * n, 128), n)


def bdot(a, b, ca, cb):
    return lax.dot_general(a, b, (((ca,), (cb,)), ((), ())), preferred_element_type=jnp.float32)


def gather_gram(x_ref, hi_ref, lo_ref, g_ref, cols, part, parts, mine, planes, s0, r0, s1, r1, s2, r2, s3, r3, ls):
    me, g = lax.axis_index("fibre"), lax.axis_index("group")
    bar = pltpu.get_barrier_semaphore()
    for t in FAR:
        pl.semaphore_signal(bar, inc=1, device_id=(peer(me, t), g), device_id_type=MESH)
    for k in range(1, NG):
        pl.semaphore_signal(bar, inc=1, device_id=(me, (g + k) % NG), device_id_type=MESH)
    pl.semaphore_wait(bar, NF + NG - 2)

    def send(src, dst, to, s, r, i):
        c = pltpu.make_async_remote_copy(
            src_ref=src, dst_ref=dst, send_sem=s.at[i], recv_sem=r.at[i], device_id=to, device_id_type=MESH
        )
        c.start()
        return c

    cs = [
        send(x_ref.at[:, lanes(peer(me, t), W)], cols.at[rows(me, 16), :], (peer(me, t), g), s0, r0, i)
        for i, t in enumerate(FAR)
    ]
    own = pltpu.make_async_copy(x_ref.at[:, lanes(me, W)], cols.at[rows(me, 16), :], ls)
    own.start()
    for c in cs:
        c.wait()
    own.wait()

    for k in range(4):
        v = cols[128 * k : 128 * k + 128, :]
        top = v.astype(jnp.bfloat16)
        hi_ref[128 * k : 128 * k + 128, :] = top
        lo_ref[128 * k : 128 * k + 128, :] = (v - top.astype(jnp.float32)).astype(jnp.bfloat16)
    for i in range(4):
        a, al = hi_ref[128 * i : 128 * i + 128, :], lo_ref[128 * i : 128 * i + 128, :]
        n = 128 * (i + 1)
        b, bl = hi_ref[0:n, :], lo_ref[0:n, :]
        blk = (bdot(a, b, 1, 1) + (bdot(a, bl, 1, 1) + bdot(al, b, 1, 1))) * (1.0 / COLS)
        for j in range(i + 1):
            o = 128 * (i * (i + 1) // 2 + j)
            part[o : o + 128, :] = blk[:, 128 * j : 128 * j + 128]

    cs = [
        send(part.at[rows(peer(me, t), OWN), :], parts.at[me], (peer(me, t), g), s1, r1, i) for i, t in enumerate(FAR)
    ]
    parts[me] = part[rows(me, OWN), :]
    for c in cs:
        c.wait()
    mine[...] = parts[0]
    for f in range(1, NF):
        mine[...] += parts[f]

    cs = [
        send(mine, planes.at[g], (me, (g + k) % NG), s2, r2, k - 1) for k in range(1, NG)
    ]
    planes[g] = mine[...]
    for c in cs:
        c.wait()
    total = planes[0]
    for f in range(1, NG):
        total = total + planes[f]
    g_ref[rows(me, OWN), :] = total

    cs = [
        send(g_ref.at[rows(me, OWN), :], g_ref.at[rows(me, OWN), :], (peer(me, t), g), s3, r3, i)
        for i, t in enumerate(FAR)
    ]
    for c in cs:
        c.wait()


def dot(a,b,ca=1,cb=0):
    return lax.dot_general(a,b,(((ca,),(cb,)),((),())),precision=HI,preferred_element_type=jnp.float32)
def diag_block(w):
    lane=lax.broadcasted_iota(jnp.int32,(8,128),1)
    sub=lax.broadcasted_iota(jnp.int32,(8,128),0)
    gather=lambda v,j:jnp.take_along_axis(v,jnp.full((8,128),j,jnp.int32),axis=1)
    spread=lambda v,r:jnp.broadcast_to(v[r:r+1,:],(8,128))
    def apply(A,W,base):
        group=(lane>=base)&(lane<base+8)
        t=[gather(A,base+r)*W[r] for r in range(8)]
        return jnp.where(group,0.0,A)-(((t[0]+t[1])+(t[2]+t[3]))+((t[4]+t[5])+(t[6]+t[7])))
    def step(p,carry):
        R,Wp=carry
        base=pl.multiple_of(8*p,8)
        kept=R
        B=[gather(R,base+c) for c in range(8)]
        for r in range(8):
            hit=lane==base+r
            row=spread(R,r)
            kept=jnp.where(sub==r,row,kept)
            inv=1.0/spread(B[r],r)
            m=B[r]*inv
            for c in range(r+1,8):
                rc=spread(B[c],r)
                B[c]=jnp.where(sub==r,rc*inv,B[c]-m*rc)
            R=jnp.where(sub==r,jnp.where(hit,1.0,row)*inv,jnp.where(hit,0.0,R)-m*jnp.where(hit,1.0,row))
        prev=jnp.maximum(base-8,0)
        Wl=[spread(Wp,r) for r in range(8)]
        for i in range(2,16):
            A=w[8*i:8*i+8,:]
            w[8*i:8*i+8,:]=jnp.where(i>p,jnp.where(p>0,apply(A,Wl,prev),A),A)
        w[pl.ds(base,8),:]=kept
        W=[spread(R,r) for r in range(8)]
        nxt=apply(w[pl.ds(base+8,8),:],W,base)
        return nxt,R
    lax.fori_loop(0,16,step,(w[0:8,:],jnp.zeros((8,128),jnp.float32)))
def chol_kernel(g_ref, l_ref, hi_ref, lo_ref, a_ref, li_ref, w):
    B=128; nb=4
    l_ref[...]=jnp.zeros((512,512),jnp.float32)
    li_ref[...]=jnp.zeros((512,512),jnp.float32)
    for i in range(4):
        for j in range(i+1):
            b = i*(i+1)//2+j
            a_ref[128*i:128*i+128,128*j:128*j+128]=g_ref[128*b:128*b+128,:]
    ri=lax.broadcasted_iota(jnp.int32,(B,B),0); ci=lax.broadcasted_iota(jnp.int32,(B,B),1)
    for k in range(nb):
        o=k*B; n=512-o-B
        w[0:B,:]=a_ref[o:o+B,o:o+B]
        diag_block(w)
        A=w[0:B,:]
        d=jnp.sum(jnp.where(ri==ci,A,0.0),axis=1,keepdims=True)
        rs=lax.rsqrt(d)
        U=jnp.where(ci>=ri,A,0.0)*rs
        LI=jnp.where(ci<ri,A,jnp.where(ri==ci,1.0,0.0))*rs
        l_ref[o:o+B,o:o+B]=U.T
        if n:
            L21=dot(a_ref[o+B:,o:o+B],LI,1,1)
            l_ref[o+B:,o:o+B]=L21
            a_ref[o+B:,o+B:]=a_ref[o+B:,o+B:]-dot(L21,L21,1,1)
        if k:
            T=dot(l_ref[o:o+B,0:o],li_ref[0:o,0:o])
            li_ref[o:o+B,0:o]=-dot(LI,T)
        li_ref[o:o+B,o:o+B]=LI
    li = li_ref[...]
    top = li.astype(jnp.bfloat16)
    hi_ref[...] = top
    lo_ref[...] = (li - top.astype(jnp.float32)).astype(jnp.bfloat16)


def solve_scatter(hi_ref, lo_ref, lh_ref, ll_ref, o_ref, buf, s, r, ls):
    me, g = lax.axis_index("fibre"), lax.axis_index("group")
    bar = pltpu.get_barrier_semaphore()
    for t in FAR:
        pl.semaphore_signal(bar, inc=1, device_id=(peer(me, t), g), device_id_type=MESH)
    cs = []
    for n, dx in enumerate((2, 1, 3, 0)):
        k = (me // 8 + dx) % 4
        lh, ll = lh_ref[rows(k, 128), :], ll_ref[rows(k, 128), :]
        hi = hi_ref[...]
        buf[rows(k, 128), :] = bdot(lh, hi, 1, 0) + (bdot(lh, lo_ref[...], 1, 0) + bdot(ll, hi, 1, 0))
        if n == 0:
            pl.semaphore_wait(bar, NF - 1)
        for i, t in enumerate(FAR):
            if t[0] == dx:
                p = peer(me, t)
                c = pltpu.make_async_remote_copy(
                    src_ref=buf.at[rows(p, 16), :],
                    dst_ref=o_ref.at[:, lanes(me, W)],
                    send_sem=s.at[i],
                    recv_sem=r.at[i],
                    device_id=(p, g),
                    device_id_type=MESH,
                )
                c.start()
                cs.append(c)
    own = pltpu.make_async_copy(buf.at[rows(me, 16), :], o_ref.at[:, lanes(me, W)], ls)
    own.start()
    for c in cs:
        c.wait()
    own.wait()


def local(tensor):
    f32, bf16, shape = jnp.float32, jnp.bfloat16, jax.ShapeDtypeStruct
    vmem, dma = pl.BlockSpec(memory_space=pltpu.VMEM), pltpu.SemaphoreType.DMA
    hi, lo, gram = pl.pallas_call(
        gather_gram,
        out_shape=(shape((M, W), bf16), shape((M, W), bf16), shape((PACK, 128), f32)),
        in_specs=[pl.BlockSpec(memory_space=pl.ANY)],
        out_specs=(vmem, vmem, vmem),
        scratch_shapes=[
            pltpu.VMEM((M, W), f32),
            pltpu.VMEM((PACK, 128), f32),
            pltpu.VMEM((NF, OWN, 128), f32),
            pltpu.VMEM((OWN, 128), f32),
            pltpu.VMEM((NG, OWN, 128), f32),
            dma((NF - 1,)),
            dma((NF - 1,)),
            dma((NF - 1,)),
            dma((NF - 1,)),
            dma((NG - 1,)),
            dma((NG - 1,)),
            dma((NF - 1,)),
            dma((NF - 1,)),
            dma,
        ],
        compiler_params=pltpu.CompilerParams(collective_id=0, has_side_effects=True, vmem_limit_bytes=32 << 20),
    )(tensor)
    factor, lh, ll = pl.pallas_call(
        chol_kernel,
        out_shape=(shape((M, M), f32), shape((M, M), bf16), shape((M, M), bf16)),
        in_specs=[vmem],
        out_specs=(vmem, vmem, vmem),
        scratch_shapes=[pltpu.VMEM((M, M), f32), pltpu.VMEM((M, M), f32), pltpu.VMEM((136, 128), f32)],
        compiler_params=pltpu.CompilerParams(vmem_limit_bytes=32 << 20),
    )(gram)
    basis = pl.pallas_call(
        solve_scatter,
        out_shape=shape(tensor.shape, f32),
        in_specs=[vmem] * 4,
        out_specs=pl.BlockSpec(memory_space=pl.ANY),
        scratch_shapes=[pltpu.VMEM((M, W), f32), dma((NF - 1,)), dma((NF - 1,)), dma],
        compiler_params=pltpu.CompilerParams(collective_id=1, has_side_effects=True, vmem_limit_bytes=32 << 20),
    )(hi, lo, lh, ll)
    return basis, factor


def solution(mesh):
    return jax.shard_map(
        local,
        mesh=mesh,
        in_specs=(P("fibre", "group"),),
        out_specs=(P("fibre", "group"), P()),
        check_vma=False,
    )
```

```python
import jax
import jax.numpy as jnp
from jax import lax
from jax.experimental import pallas as pl
from jax.experimental.pallas import tpu as pltpu
from jax.sharding import PartitionSpec as P

HI = lax.Precision.HIGHEST
MESH = pl.DeviceIdType.MESH
M = 512
NF = 32
NG = 8
W = 1536
COLS = W * NF * NG
PACK = 1280
OWN = PACK // NF
HALF = PACK // 2
CHUNKS = ((0, 24), (24, 16))
CHIPS = sorted(
    [(dx, dy) for dx in range(4) for dy in range(4) if (dx, dy) != (0, 0)],
    key=lambda t: -(min(t[0], 4 - t[0]) + min(t[1], 4 - t[1])),
)
FAR = sorted(
    [(dx, dy, dc) for dx in range(4) for dy in range(4) for dc in range(2) if (dx, dy, dc) != (0, 0, 0)],
    key=lambda t: -(min(t[0], 4 - t[0]) + min(t[1], 4 - t[1])),
)


def peer(me, t):
    x, y, c = me // 8, (me // 2) % 4, me % 2
    return ((x + t[0]) % 4 * 4 + (y + t[1]) % 4) * 2 + (c + t[2]) % 2


def chip(x, y, c):
    return ((x % 4) * 4 + y % 4) * 2 + c % 2


def exchange(pair, one, slot, slot_one, dst, sems, local_sem, order=(2, 1, 3), hook=None):
    s1, r1, s2, r2 = sems
    me, g = lax.axis_index("fibre"), lax.axis_index("group")
    x, y, c = me // 8, (me // 2) % 4, me % 2
    first, last, own = {}, [], []

    def go(h, d, e, dc, src, f):
        to = chip(x, y + e, c + dc) if h == 0 else chip(x + e, y, c + dc)
        if e == 0 and dc == 0:
            k = pltpu.make_async_copy(src, dst(h, f), local_sem.at[h, d])
            own.append(k)
        else:
            k = pltpu.make_async_remote_copy(
                src_ref=src, dst_ref=dst(h, f), send_sem=s2.at[h, d, e, dc], recv_sem=r2.at[h, d, e, dc],
                device_id=(to, g), device_id_type=MESH,
            )
            last.append(k)
        k.start()

    for h, d, e in (
        [(h, d, e) for d in order for e in (2, 1, 3, 0) for h in range(2)]
        if hook is None
        else [(h, d, e) for h in range(2) for d in order for e in (2, 1, 3, 0)]
    ):
                if hook is not None and (d, e) == (order[0], 2):
                    hook(h)
                X, Y = (x + d, y + e) if h == 0 else (x + e, y + d)
                to = chip(x + d, y, c) if h == 0 else chip(x, y + d, c)
                k = pltpu.make_async_remote_copy(
                    src_ref=pair(h, X % 4, Y % 4), dst_ref=slot(h, d, e), send_sem=s1.at[h, d, e],
                    recv_sem=r1.at[h, d, e], device_id=(to, g), device_id_type=MESH,
                )
                k.start()
                first[h, d, e] = k
    for e in (2, 1, 3, 0):
        for dc in range(2):
            for h in range(2):
                X, Y = (x, y + e) if h == 0 else (x + e, y)
                go(h, 0, e, dc, one(h, X % 4, Y % 4, (c + dc) % 2), me)
    for d in order:
        for e in (2, 1, 3, 0):
            for h in range(2):
                first[h, d, e].wait_recv()
                f = chip(x - d + 4, y, c) if h == 0 else chip(x, y - d + 4, c)
                for dc in range(2):
                    go(h, d, e, dc, slot_one(h, d, e, (c + dc) % 2), f)
    for k in first.values():
        k.wait_send()
    for k in last + own:
        k.wait()


def cross(me):
    x, y, c = me // 8, (me // 2) % 4, me % 2
    t = [(0, 0, 1)] + [(d, 0, k) for d in (1, 2, 3) for k in (0, 1)] + [(0, d, k) for d in (1, 2, 3) for k in (0, 1)]
    return [chip(x + a, y + b, c + k) for a, b, k in t]


def rows(i, n):
    return pl.ds(pl.multiple_of(i * n, 8), n)


def lanes(i, n):
    return pl.ds(pl.multiple_of(i * n, 128), n)


def bdot(a, b, ca, cb):
    return lax.dot_general(a, b, (((ca,), (cb,)), ((), ())), preferred_element_type=jnp.float32)


def gather_gram(x_ref, hi_ref, lo_ref, g_ref, cols, relay, part, pair, keep, parts, mine, planes, sa, ra, sb, rb, ls,
                s0, r0, s1, r1, s2, r2, s3, r3, s4, r4):
    me, g = lax.axis_index("fibre"), lax.axis_index("group")
    bar = pltpu.get_barrier_semaphore()
    for t in FAR:
        pl.semaphore_signal(bar, inc=1, device_id=(peer(me, t), g), device_id_type=MESH)
    for k in range(1, NG):
        pl.semaphore_signal(bar, inc=1, device_id=(me, (g + k) % NG), device_id_type=MESH)
    pl.semaphore_wait(bar, NF + NG - 2)

    def send(src, dst, to, s, r, i):
        c = pltpu.make_async_remote_copy(
            src_ref=src, dst_ref=dst, send_sem=s.at[i], recv_sem=r.at[i], device_id=to, device_id_type=MESH
        )
        c.start()
        return c

    exchange(
        lambda h, X, Y: x_ref.at[8 * h : 8 * h + 8, lanes(X * 4 + Y, 2 * W)],
        lambda h, X, Y, C: x_ref.at[8 * h : 8 * h + 8, lanes((X * 4 + Y) * 2 + C, W)],
        lambda h, d, e: relay.at[h, d - 1, e],
        lambda h, d, e, C: relay.at[h, d - 1, e, :, lanes(C, W)],
        lambda h, f: cols.at[rows(2 * f + h, 8), :],
        (sa, ra, sb, rb),
        ls,
    )

    for k in range(4):
        v = cols[128 * k : 128 * k + 128, :]
        top = v.astype(jnp.bfloat16)
        hi_ref[128 * k : 128 * k + 128, :] = top
        lo_ref[128 * k : 128 * k + 128, :] = (v - top.astype(jnp.float32)).astype(jnp.bfloat16)
    for i in range(4):
        a, al = hi_ref[128 * i : 128 * i + 128, :], lo_ref[128 * i : 128 * i + 128, :]
        n = 128 * (i + 1)
        b, bl = hi_ref[0:n, :], lo_ref[0:n, :]
        blk = (bdot(a, b, 1, 1) + (bdot(a, bl, 1, 1) + bdot(al, b, 1, 1))) * (1.0 / COLS)
        for j in range(i + 1):
            o = 128 * (i * (i + 1) // 2 + j)
            part[o : o + 128, :] = blk[:, 128 * j : 128 * j + 128]

    x, y, c = me // 8, (me // 2) % 4, me % 2
    p, twin = me // 2, (chip(x, y, c + 1), g)
    ks = range(len(CHUNKS))

    def span(core, k):
        return pl.ds(pl.multiple_of(core * HALF + 16 * CHUNKS[k][0], 8), 16 * CHUNKS[k][1])

    def piece(core, k, q):
        return pl.ds(pl.multiple_of(core * HALF + 16 * CHUNKS[k][0] + q * CHUNKS[k][1], 8), CHUNKS[k][1])

    def near(k):
        return pl.ds(16 * CHUNKS[k][0], 16 * CHUNKS[k][1])

    swap = [send(part.at[span(1 - c, k), :], pair.at[near(k), :], twin, s0, r0, k) for k in ks]
    plane = []
    for k in ks:
        swap[k].wait_recv()
        keep[near(k), :] = part[span(c, k), :] + pair[near(k), :]
        o, n = CHUNKS[k]
        cs = []
        for i, t in enumerate(CHIPS):
            q = chip(x + t[0], y + t[1], c)
            src = keep.at[pl.ds(pl.multiple_of(16 * o + (q // 2) * n, 8), n), :]
            cs.append(send(src, parts.at[p, o : o + n, :], (q, g), s1, r1, 15 * k + i))
        parts[p, o : o + n, :] = keep[pl.ds(pl.multiple_of(16 * o + p * n, 8), n), :]
        plane.append(cs)

    def added(ref, count, o, n):
        v = [ref[f, o : o + n, :] for f in range(count)]
        while len(v) > 1:
            v = [v[f] + v[f + 1] for f in range(0, len(v), 2)]
        return v[0]

    depth = []
    for k in ks:
        o, n = CHUNKS[k]
        for q in plane[k]:
            q.wait_recv()
        mine[o : o + n, :] = added(parts, NF // 2, o, n)
        depth.append([
            send(mine.at[o : o + n, :], planes.at[g, o : o + n, :], (me, (g + d) % NG), s2, r2, 7 * k + d - 1)
            for d in (4, 3, 5, 2, 6, 1, 7)
        ])
        planes[g, o : o + n, :] = mine[o : o + n, :]

    spread, over = [], []
    for k in ks:
        o, n = CHUNKS[k]
        for q in depth[k]:
            q.wait_recv()
        g_ref[piece(c, k, p), :] = added(planes, NG, o, n)
        own = g_ref.at[piece(c, k, p), :]
        spread.append([
            send(own, own, (chip(x + t[0], y + t[1], c), g), s3, r3, 15 * k + i) for i, t in enumerate(CHIPS)
        ])
        over.append(send(own, own, twin, s4, r4, 16 * k + 15))
    for k in ks:
        for i in reversed(range(15)):
            t = CHIPS[i]
            spread[k][i].wait_recv()
            got = g_ref.at[piece(c, k, chip(x - t[0] + 4, y - t[1] + 4, 0) // 2), :]
            over.append(send(got, got, twin, s4, r4, 16 * k + i))
    for q in swap + [q for l in plane + depth + spread for q in l]:
        q.wait_send()
    for q in over:
        q.wait()


def dot(a,b,ca=1,cb=0):
    return lax.dot_general(a,b,(((ca,),(cb,)),((),())),precision=HI,preferred_element_type=jnp.float32)
def diag_block(w):
    lane=lax.broadcasted_iota(jnp.int32,(8,128),1)
    sub=lax.broadcasted_iota(jnp.int32,(8,128),0)
    spread=lambda v,r:jnp.broadcast_to(v[r:r+1,:],(8,128))
    def gather(v,base,r):
        return jnp.take_along_axis(v,jnp.full((8,128),jnp.clip(base+r,0,127),jnp.int32),axis=1)
    def total(t):
        return ((t[0]+t[1])+(t[2]+t[3]))+((t[4]+t[5])+(t[6]+t[7]))
    def apply(A,C,W,base):
        group=(lane>=base)&(lane<base+8)
        return jnp.where(group,0.0,A)-total([C[r]*W[r] for r in range(8)])
    rowf=lax.broadcasted_iota(jnp.int32,(128,128),0)
    def make(lo):
      def step(p,carry):
        R,Q,Wp=carry
        base=pl.multiple_of(8*p,8)
        prev=base-8
        B=[gather(R,base,c) for c in range(8)]
        C=[gather(Q,base,r) for r in range(8)]
        S=w[pl.ds(base+16,8),:]
        G1=[gather(S,prev,r) for r in range(8)]
        Wl=[spread(Wp,r) for r in range(8)]
        S=apply(S,G1,Wl,prev)
        G2=[gather(S,base,r) for r in range(8)]
        A=w[8*lo:128,:]
        rowi=lax.broadcasted_iota(jnp.int32,A.shape,0)+8*lo
        lan=lax.broadcasted_iota(jnp.int32,A.shape,1)
        full=jnp.where((rowf>=prev)&(rowf<base),jnp.concatenate([Wp]*16,axis=0),0.0)
        N=jnp.where((lan>=prev)&(lan<base),0.0,A)-dot(A,full)
        w[8*lo:128,:]=jnp.where(rowi>=8*p+24,N,A)
        kept=R
        for r in range(8):
            here=sub==r
            row=spread(R,r)
            kept=jnp.where(here,row,kept)
            inv=1.0/spread(B[r],r)
            m=B[r]*inv
            for c in range(r+1,8):
                rc=spread(B[c],r)
                B[c]=jnp.where(here,rc*inv,B[c]-m*rc)
            hit=lane==base+r
            row=jnp.where(hit,1.0,row)
            R=jnp.where(here,row*inv,jnp.where(hit,0.0,R)-m*row)
        W=[spread(R,r) for r in range(8)]
        newR=apply(Q,C,W,base)
        newQ=apply(S,G2,W,base)
        w[pl.ds(base,8),:]=kept
        return newR,newQ,R
      return step
    carry=(w[0:8,:],w[8:16,:],jnp.zeros((8,128),jnp.float32))
    carry=lax.fori_loop(0,8,make(3),carry)
    lax.fori_loop(8,16,make(11),carry)
def factor_solve_scatter(
    g_ref, hi_ref, lo_ref, l_ref, o_ref, a_ref, li_ref, w, buf, relay, sa, ra, sb, rb, ls
):
    me, g = lax.axis_index("fibre"), lax.axis_index("group")
    x, y, c = me // 8, (me // 2) % 4, me % 2
    bar = pltpu.get_barrier_semaphore()
    targets = cross(me)
    for t in targets:
        pl.semaphore_signal(bar, inc=1, device_id=(t, g), device_id_type=MESH)

    def first(h, d, e):
        X, Y = (x + d, y + e) if h == 0 else (x + e, y + d)
        to = chip(x + d, y, c) if h == 0 else chip(x, y + d, c)
        return pltpu.make_async_remote_copy(
            src_ref=buf.at[h, rows((X % 4) * 4 + Y % 4, 16), :],
            dst_ref=relay.at[h, d, e],
            send_sem=sa.at[h, d, e],
            recv_sem=ra.at[h, d, e],
            device_id=(to, g),
            device_id_type=MESH,
        )

    def place(h, d, e, dc):
        X, Y = (x, y + e) if h == 0 else (x + e, y)
        C = (c + dc) % 2
        if d == 0:
            src, f = buf.at[h, rows(((X % 4) * 4 + Y % 4) * 2 + C, 8), :], me
        else:
            src = relay.at[h, d, e, rows(C, 8), :]
            f = chip(x - d + 4, y, c) if h == 0 else chip(x, y - d + 4, c)
        return src, o_ref.at[8 * h : 8 * h + 8, lanes(f, W)], (chip(X, Y, C), g)

    def last(h, d, e, dc):
        src, dst, to = place(h, d, e, dc)
        return pltpu.make_async_remote_copy(
            src_ref=src, dst_ref=dst, send_sem=sb.at[h, d, e, dc], recv_sem=rb.at[h, d, e, dc],
            device_id=to, device_id_type=MESH,
        )

    def stay(h, d, e):
        src, dst, to = place(h, d, e, 0)
        return pltpu.make_async_copy(src, dst, ls.at[h, d])

    def go(h, d, e):
        last(h, d, e, 1).start()
        if h == 0:
            if e == 0:
                stay(h, d, e).start()
            else:
                last(h, d, e, 0).start()
        else:
            pl.when(e == 0)(lambda: stay(h, d, e).start())
            pl.when(e != 0)(lambda: last(h, d, e, 0).start())

    def post(k):
        off = (k - x + 4) % 4

        @pl.when(off != 0)
        def _():
            for e in (2, 1, 3, 0):
                first(0, off, e).start()

        @pl.when(off == 0)
        def _():
            for e in (2, 1, 3, 0):
                go(0, 0, e)

        for d in (2, 1, 3):
            first(1, d, off).start()
        go(1, 0, off)

    def forward(k):
        off = (k - x + 4) % 4
        for d in (2, 1, 3):
            first(1, d, off).wait_recv()
            go(1, d, off)

        @pl.when(off == 0)
        def _():
            for d in (2, 1, 3):
                for e in (2, 1, 3, 0):
                    first(0, d, e).wait_recv()
                    go(0, d, e)

    l_ref[...] = jnp.zeros((M, M), jnp.float32)
    li_ref[...] = jnp.zeros((M, M), jnp.float32)
    B = 128
    for i in range(4):
        for j in range(i + 1):
            b = i * (i + 1) // 2 + j
            a_ref[B * i : B * i + B, B * j : B * j + B] = g_ref[B * b : B * b + B, :]
    ri = lax.broadcasted_iota(jnp.int32, (B, B), 0)
    ci = lax.broadcasted_iota(jnp.int32, (B, B), 1)
    for k in range(4):
        o, n = k * B, (k + 1) * B
        w[0:B, :] = a_ref[o:n, o:n]
        diag_block(w)
        A = w[0:B, :]
        rs = lax.rsqrt(jnp.sum(jnp.where(ri == ci, A, 0.0), axis=1, keepdims=True))
        U = jnp.where(ci >= ri, A, 0.0) * rs
        LI = jnp.where(ci < ri, A, jnp.where(ri == ci, 1.0, 0.0)) * rs
        l_ref[o:n, o:n] = U.T
        if k:
            li_ref[o:n, 0:o] = -dot(LI, dot(l_ref[o:n, 0:o], li_ref[0:o, 0:o]))
        li_ref[o:n, o:n] = LI
        li = li_ref[o:n, 0:n].reshape(8, 2, 8, n)
        li = jnp.concatenate([li[:, 0].reshape(64, n), li[:, 1].reshape(64, n)], axis=0)
        lh = li.astype(jnp.bfloat16)
        ll = (li - lh.astype(jnp.float32)).astype(jnp.bfloat16)
        hi = hi_ref[0:n, :]
        X = bdot(lh, hi, 1, 0) + (bdot(lh, lo_ref[0:n, :], 1, 0) + bdot(ll, hi, 1, 0))
        buf[0, 64 * k : 64 * k + 64, :] = X[0:64]
        buf[1, 64 * k : 64 * k + 64, :] = X[64:128]
        if k == 0:
            pl.semaphore_wait(bar, len(targets))
        post(k)
        if k >= 2:
            forward(k - 2)
        if k < 3:
            L21 = dot(a_ref[n:, o:n], LI, 1, 1)
            l_ref[n:, o:n] = L21
            a_ref[n:, n:] = a_ref[n:, n:] - dot(L21, L21, 1, 1)
    forward(2)
    forward(3)
    for h in range(2):
        for d in range(4):
            for e in range(4):
                if d:
                    first(h, d, e).wait_send()
                last(h, d, e, 1).wait()
                if e:
                    last(h, d, e, 0).wait()
            stay(h, d, 0).wait()


def local(tensor):
    f32, bf16, shape = jnp.float32, jnp.bfloat16, jax.ShapeDtypeStruct
    hops = [
        pltpu.SemaphoreType.DMA(n)
        for n in ((2, 4, 4), (2, 4, 4), (2, 4, 4, 2), (2, 4, 4, 2), (2, 4))
    ]
    vmem, dma = pl.BlockSpec(memory_space=pltpu.VMEM), pltpu.SemaphoreType.DMA
    hi, lo, gram = pl.pallas_call(
        gather_gram,
        out_shape=(shape((M, W), bf16), shape((M, W), bf16), shape((PACK, 128), f32)),
        in_specs=[pl.BlockSpec(memory_space=pl.ANY)],
        out_specs=(vmem, vmem, vmem),
        scratch_shapes=[
            pltpu.VMEM((M, W), f32),
            pltpu.VMEM((2, 3, 4, 8, 2 * W), f32),
            pltpu.VMEM((PACK, 128), f32),
            pltpu.VMEM((HALF, 128), f32),
            pltpu.VMEM((HALF, 128), f32),
            pltpu.VMEM((NF // 2, OWN, 128), f32),
            pltpu.VMEM((OWN, 128), f32),
            pltpu.VMEM((NG, OWN, 128), f32),
            *hops,
            dma((2,)),
            dma((2,)),
            dma((30,)),
            dma((30,)),
            dma((14,)),
            dma((14,)),
            dma((30,)),
            dma((30,)),
            dma((32,)),
            dma((32,)),
        ],
        compiler_params=pltpu.CompilerParams(collective_id=0, has_side_effects=True, vmem_limit_bytes=32 << 20),
    )(tensor)
    factor, basis = pl.pallas_call(
        factor_solve_scatter,
        out_shape=(shape((M, M), f32), shape(tensor.shape, f32)),
        in_specs=[vmem] * 3,
        out_specs=(vmem, pl.BlockSpec(memory_space=pl.ANY)),
        scratch_shapes=[
            pltpu.VMEM((M, M), f32),
            pltpu.VMEM((M, M), f32),
            pltpu.VMEM((144, 128), f32),
            pltpu.VMEM((2, M // 2, W), f32),
            pltpu.VMEM((2, 4, 4, 16, W), f32),
            *hops,
        ],
        compiler_params=pltpu.CompilerParams(collective_id=1, has_side_effects=True, vmem_limit_bytes=32 << 20),
    )(gram, hi, lo)
    return basis, factor


def solution(mesh):
    return jax.shard_map(
        local,
        mesh=mesh,
        in_specs=(P("fibre", "group"),),
        out_specs=(P("fibre", "group"), P()),
        check_vma=False,
    )
```

```python
import jax
import jax.numpy as jnp
from jax import lax
from jax.experimental import pallas as pl
from jax.experimental.pallas import tpu as pltpu
from jax.sharding import PartitionSpec as P

HI = lax.Precision.HIGHEST
MESH = pl.DeviceIdType.MESH
M = 512
NF = 32
NG = 8
W = 1536
COLS = W * NF * NG
PACK = 1280
OWN = PACK // NF
HALF = PACK // 2
CHUNKS = ((0, 24), (24, 16))
CHIPS = sorted(
    [(dx, dy) for dx in range(4) for dy in range(4) if (dx, dy) != (0, 0)],
    key=lambda t: -(min(t[0], 4 - t[0]) + min(t[1], 4 - t[1])),
)
FAR = sorted(
    [(dx, dy, dc) for dx in range(4) for dy in range(4) for dc in range(2) if (dx, dy, dc) != (0, 0, 0)],
    key=lambda t: -(min(t[0], 4 - t[0]) + min(t[1], 4 - t[1])),
)


def peer(me, t):
    x, y, c = me // 8, (me // 2) % 4, me % 2
    return ((x + t[0]) % 4 * 4 + (y + t[1]) % 4) * 2 + (c + t[2]) % 2


def chip(x, y, c):
    return ((x % 4) * 4 + y % 4) * 2 + c % 2


def exchange(pair, one, slot, slot_one, dst, sems, local_sem, order=(2, 1, 3), hook=None):
    s1, r1, s2, r2 = sems
    me, g = lax.axis_index("fibre"), lax.axis_index("group")
    x, y, c = me // 8, (me // 2) % 4, me % 2
    first, last, own = {}, [], []

    def go(h, d, e, dc, src, f):
        to = chip(x, y + e, c + dc) if h == 0 else chip(x + e, y, c + dc)
        if e == 0 and dc == 0:
            k = pltpu.make_async_copy(src, dst(h, f), local_sem.at[h, d])
            own.append(k)
        else:
            k = pltpu.make_async_remote_copy(
                src_ref=src, dst_ref=dst(h, f), send_sem=s2.at[h, d, e, dc], recv_sem=r2.at[h, d, e, dc],
                device_id=(to, g), device_id_type=MESH,
            )
            last.append(k)
        k.start()

    for h, d, e in (
        [(h, d, e) for d in order for e in (2, 1, 3, 0) for h in range(2)]
        if hook is None
        else [(h, d, e) for h in range(2) for d in order for e in (2, 1, 3, 0)]
    ):
                if hook is not None and (d, e) == (order[0], 2):
                    hook(h)
                X, Y = (x + d, y + e) if h == 0 else (x + e, y + d)
                to = chip(x + d, y, c) if h == 0 else chip(x, y + d, c)
                k = pltpu.make_async_remote_copy(
                    src_ref=pair(h, X % 4, Y % 4), dst_ref=slot(h, d, e), send_sem=s1.at[h, d, e],
                    recv_sem=r1.at[h, d, e], device_id=(to, g), device_id_type=MESH,
                )
                k.start()
                first[h, d, e] = k
    for e in (2, 1, 3, 0):
        for dc in range(2):
            for h in range(2):
                X, Y = (x, y + e) if h == 0 else (x + e, y)
                go(h, 0, e, dc, one(h, X % 4, Y % 4, (c + dc) % 2), me)
    for d in order:
        for e in (2, 1, 3, 0):
            for h in range(2):
                first[h, d, e].wait_recv()
                f = chip(x - d + 4, y, c) if h == 0 else chip(x, y - d + 4, c)
                for dc in range(2):
                    go(h, d, e, dc, slot_one(h, d, e, (c + dc) % 2), f)
    for k in first.values():
        k.wait_send()
    for k in last + own:
        k.wait()


def cross(me):
    x, y, c = me // 8, (me // 2) % 4, me % 2
    t = [(0, 0, 1)] + [(d, 0, k) for d in (1, 2, 3) for k in (0, 1)] + [(0, d, k) for d in (1, 2, 3) for k in (0, 1)]
    return [chip(x + a, y + b, c + k) for a, b, k in t]


def rows(i, n):
    return pl.ds(pl.multiple_of(i * n, 8), n)


def lanes(i, n):
    return pl.ds(pl.multiple_of(i * n, 128), n)


def bdot(a, b, ca, cb):
    return lax.dot_general(a, b, (((ca,), (cb,)), ((), ())), preferred_element_type=jnp.float32)


def gather_gram(x_ref, hi_ref, lo_ref, g_ref, cols, relay, part, pair, keep, parts, mine, planes, sa, ra, sb, rb, ls,
                s0, r0, s1, r1, s2, r2, s3, r3, s4, r4):
    me, g = lax.axis_index("fibre"), lax.axis_index("group")
    bar = pltpu.get_barrier_semaphore()
    for t in FAR:
        pl.semaphore_signal(bar, inc=1, device_id=(peer(me, t), g), device_id_type=MESH)
    for k in range(1, NG):
        pl.semaphore_signal(bar, inc=1, device_id=(me, (g + k) % NG), device_id_type=MESH)
    pl.semaphore_wait(bar, NF + NG - 2)

    def send(src, dst, to, s, r, i):
        c = pltpu.make_async_remote_copy(
            src_ref=src, dst_ref=dst, send_sem=s.at[i], recv_sem=r.at[i], device_id=to, device_id_type=MESH
        )
        c.start()
        return c

    exchange(
        lambda h, X, Y: x_ref.at[8 * h : 8 * h + 8, lanes(X * 4 + Y, 2 * W)],
        lambda h, X, Y, C: x_ref.at[8 * h : 8 * h + 8, lanes((X * 4 + Y) * 2 + C, W)],
        lambda h, d, e: relay.at[h, d - 1, e],
        lambda h, d, e, C: relay.at[h, d - 1, e, :, lanes(C, W)],
        lambda h, f: cols.at[rows(2 * f + h, 8), :],
        (sa, ra, sb, rb),
        ls,
    )

    for k in range(4):
        v = cols[128 * k : 128 * k + 128, :]
        top = v.astype(jnp.bfloat16)
        hi_ref[128 * k : 128 * k + 128, :] = top
        lo_ref[128 * k : 128 * k + 128, :] = (v - top.astype(jnp.float32)).astype(jnp.bfloat16)
    for i in range(2):
        n = 256 * (i + 1)
        a = hi_ref[n - 256 : n, :]
        both = jnp.concatenate([a, lo_ref[n - 256 : n, :]], axis=0)
        top = bdot(both, hi_ref[0:n, :], 1, 1)
        blk = (top[0:256] + (top[256:512] + bdot(a, lo_ref[0:n, :], 1, 1))) * (1.0 / COLS)
        for r in range(2):
            for j in range(2 * i + r + 1):
                o = 128 * ((2 * i + r) * (2 * i + r + 1) // 2 + j)
                part[o : o + 128, :] = blk[128 * r : 128 * r + 128, 128 * j : 128 * j + 128]

    x, y, c = me // 8, (me // 2) % 4, me % 2
    p, twin = me // 2, (chip(x, y, c + 1), g)
    ks = range(len(CHUNKS))

    def span(core, k):
        return pl.ds(pl.multiple_of(core * HALF + 16 * CHUNKS[k][0], 8), 16 * CHUNKS[k][1])

    def piece(core, k, q):
        return pl.ds(pl.multiple_of(core * HALF + 16 * CHUNKS[k][0] + q * CHUNKS[k][1], 8), CHUNKS[k][1])

    def near(k):
        return pl.ds(16 * CHUNKS[k][0], 16 * CHUNKS[k][1])

    swap = [send(part.at[span(1 - c, k), :], pair.at[near(k), :], twin, s0, r0, k) for k in ks]
    plane = []
    for k in ks:
        swap[k].wait_recv()
        keep[near(k), :] = part[span(c, k), :] + pair[near(k), :]
        o, n = CHUNKS[k]
        cs = []
        for i, t in enumerate(CHIPS):
            q = chip(x + t[0], y + t[1], c)
            src = keep.at[pl.ds(pl.multiple_of(16 * o + (q // 2) * n, 8), n), :]
            cs.append(send(src, parts.at[p, o : o + n, :], (q, g), s1, r1, 15 * k + i))
        parts[p, o : o + n, :] = keep[pl.ds(pl.multiple_of(16 * o + p * n, 8), n), :]
        plane.append(cs)

    def added(ref, count, o, n):
        v = [ref[f, o : o + n, :] for f in range(count)]
        while len(v) > 1:
            v = [v[f] + v[f + 1] for f in range(0, len(v), 2)]
        return v[0]

    depth = []
    for k in ks:
        o, n = CHUNKS[k]
        for q in plane[k]:
            q.wait_recv()
        mine[o : o + n, :] = added(parts, NF // 2, o, n)
        depth.append([
            send(mine.at[o : o + n, :], planes.at[g, o : o + n, :], (me, (g + d) % NG), s2, r2, 7 * k + d - 1)
            for d in (4, 3, 5, 2, 6, 1, 7)
        ])
        planes[g, o : o + n, :] = mine[o : o + n, :]

    spread, over = [], []
    for k in ks:
        o, n = CHUNKS[k]
        for q in depth[k]:
            q.wait_recv()
        g_ref[piece(c, k, p), :] = added(planes, NG, o, n)
        own = g_ref.at[piece(c, k, p), :]
        spread.append([
            send(own, own, (chip(x + t[0], y + t[1], c), g), s3, r3, 15 * k + i) for i, t in enumerate(CHIPS)
        ])
        over.append(send(own, own, twin, s4, r4, 16 * k + 15))
    for k in ks:
        for i in reversed(range(15)):
            t = CHIPS[i]
            spread[k][i].wait_recv()
            got = g_ref.at[piece(c, k, chip(x - t[0] + 4, y - t[1] + 4, 0) // 2), :]
            over.append(send(got, got, twin, s4, r4, 16 * k + i))
    for q in swap + [q for l in plane + depth + spread for q in l]:
        q.wait_send()
    for q in over:
        q.wait()


def dot(a,b,ca=1,cb=0):
    return lax.dot_general(a,b,(((ca,),(cb,)),((),())),precision=HI,preferred_element_type=jnp.float32)
def diag_block(w):
    lane=lax.broadcasted_iota(jnp.int32,(8,128),1)
    sub=lax.broadcasted_iota(jnp.int32,(8,128),0)
    spread=lambda v,r:jnp.broadcast_to(v[r:r+1,:],(8,128))
    def gather(v,base,r):
        return jnp.take_along_axis(v,jnp.full((8,128),jnp.clip(base+r,0,127),jnp.int32),axis=1)
    def total(t):
        return ((t[0]+t[1])+(t[2]+t[3]))+((t[4]+t[5])+(t[6]+t[7]))
    def apply(A,C,W,base):
        group=(lane>=base)&(lane<base+8)
        return jnp.where(group,0.0,A)-total([C[r]*W[r] for r in range(8)])
    rowf=lax.broadcasted_iota(jnp.int32,(128,128),0)
    def make(lo):
      def step(p,carry):
        R,Q,Wp=carry
        base=pl.multiple_of(8*p,8)
        prev=base-8
        B=[gather(R,base,c) for c in range(8)]
        C=[gather(Q,base,r) for r in range(8)]
        S=w[pl.ds(base+16,8),:]
        G1=[gather(S,prev,r) for r in range(8)]
        Wl=[spread(Wp,r) for r in range(8)]
        S=apply(S,G1,Wl,prev)
        G2=[gather(S,base,r) for r in range(8)]
        A=w[8*lo:128,:]
        rowi=lax.broadcasted_iota(jnp.int32,A.shape,0)+8*lo
        lan=lax.broadcasted_iota(jnp.int32,A.shape,1)
        full=jnp.where((rowf>=prev)&(rowf<base),jnp.concatenate([Wp]*16,axis=0),0.0)
        N=jnp.where((lan>=prev)&(lan<base),0.0,A)-dot(A,full)
        w[8*lo:128,:]=jnp.where(rowi>=8*p+24,N,A)
        kept=R
        for r in range(8):
            here=sub==r
            row=spread(R,r)
            kept=jnp.where(here,row,kept)
            inv=1.0/spread(B[r],r)
            m=B[r]*inv
            for c in range(r+1,8):
                rc=spread(B[c],r)
                B[c]=jnp.where(here,rc*inv,B[c]-m*rc)
            hit=lane==base+r
            row=jnp.where(hit,1.0,row)
            R=jnp.where(here,row*inv,jnp.where(hit,0.0,R)-m*row)
        W=[spread(R,r) for r in range(8)]
        newR=apply(Q,C,W,base)
        newQ=apply(S,G2,W,base)
        w[pl.ds(base,8),:]=kept
        return newR,newQ,R
      return step
    carry=(w[0:8,:],w[8:16,:],jnp.zeros((8,128),jnp.float32))
    carry=lax.fori_loop(0,8,make(3),carry)
    lax.fori_loop(8,16,make(11),carry)
def factor_solve_scatter(
    g_ref, hi_ref, lo_ref, l_ref, o_ref, a_ref, li_ref, w, buf, relay, sa, ra, sb, rb, ls
):
    me, g = lax.axis_index("fibre"), lax.axis_index("group")
    x, y, c = me // 8, (me // 2) % 4, me % 2
    bar = pltpu.get_barrier_semaphore()
    targets = cross(me)
    for t in targets:
        pl.semaphore_signal(bar, inc=1, device_id=(t, g), device_id_type=MESH)

    def first(h, d, e):
        X, Y = (x + d, y + e) if h == 0 else (x + e, y + d)
        to = chip(x + d, y, c) if h == 0 else chip(x, y + d, c)
        return pltpu.make_async_remote_copy(
            src_ref=buf.at[h, rows((X % 4) * 4 + Y % 4, 16), :],
            dst_ref=relay.at[h, d, e],
            send_sem=sa.at[h, d, e],
            recv_sem=ra.at[h, d, e],
            device_id=(to, g),
            device_id_type=MESH,
        )

    def place(h, d, e, dc):
        X, Y = (x, y + e) if h == 0 else (x + e, y)
        C = (c + dc) % 2
        if d == 0:
            src, f = buf.at[h, rows(((X % 4) * 4 + Y % 4) * 2 + C, 8), :], me
        else:
            src = relay.at[h, d, e, rows(C, 8), :]
            f = chip(x - d + 4, y, c) if h == 0 else chip(x, y - d + 4, c)
        return src, o_ref.at[8 * h : 8 * h + 8, lanes(f, W)], (chip(X, Y, C), g)

    def last(h, d, e, dc):
        src, dst, to = place(h, d, e, dc)
        return pltpu.make_async_remote_copy(
            src_ref=src, dst_ref=dst, send_sem=sb.at[h, d, e, dc], recv_sem=rb.at[h, d, e, dc],
            device_id=to, device_id_type=MESH,
        )

    def stay(h, d, e):
        src, dst, to = place(h, d, e, 0)
        return pltpu.make_async_copy(src, dst, ls.at[h, d])

    def go(h, d, e):
        last(h, d, e, 1).start()
        if h == 0:
            if e == 0:
                stay(h, d, e).start()
            else:
                last(h, d, e, 0).start()
        else:
            pl.when(e == 0)(lambda: stay(h, d, e).start())
            pl.when(e != 0)(lambda: last(h, d, e, 0).start())

    def post(k):
        off = (k - x + 4) % 4

        @pl.when(off != 0)
        def _():
            for e in (2, 1, 3, 0):
                first(0, off, e).start()

        @pl.when(off == 0)
        def _():
            for e in (2, 1, 3, 0):
                go(0, 0, e)

        for d in (2, 1, 3):
            first(1, d, off).start()
        go(1, 0, off)

    def turn_x(k):
        off = (k - x + 4) % 4
        for d in (2, 1, 3):
            first(1, d, off).wait_recv()
            go(1, d, off)

    def turn_y():
        for d in (2, 1, 3):
            for e in (2, 1, 3, 0):
                first(0, d, e).wait_recv()
                go(0, d, e)

    l_ref[...] = jnp.zeros((M, M), jnp.float32)
    li_ref[...] = jnp.zeros((M, M), jnp.float32)
    B = 128
    for i in range(4):
        for j in range(i + 1):
            b = i * (i + 1) // 2 + j
            a_ref[B * i : B * i + B, B * j : B * j + B] = g_ref[B * b : B * b + B, :]
    ri = lax.broadcasted_iota(jnp.int32, (B, B), 0)
    ci = lax.broadcasted_iota(jnp.int32, (B, B), 1)
    for k in range(4):
        o, n = k * B, (k + 1) * B
        w[0:B, :] = a_ref[o:n, o:n]
        diag_block(w)
        A = w[0:B, :]
        rs = lax.rsqrt(jnp.sum(jnp.where(ri == ci, A, 0.0), axis=1, keepdims=True))
        U = jnp.where(ci >= ri, A, 0.0) * rs
        LI = jnp.where(ci < ri, A, jnp.where(ri == ci, 1.0, 0.0)) * rs
        l_ref[o:n, o:n] = U.T
        if k:
            li_ref[o:n, 0:o] = -dot(LI, dot(l_ref[o:n, 0:o], li_ref[0:o, 0:o]))
        li_ref[o:n, o:n] = LI
        li = li_ref[o:n, 0:n].reshape(8, 2, 8, n)
        li = jnp.concatenate([li[:, 0].reshape(64, n), li[:, 1].reshape(64, n)], axis=0)
        lh = li.astype(jnp.bfloat16)
        ll = (li - lh.astype(jnp.float32)).astype(jnp.bfloat16)
        top = bdot(jnp.concatenate([lh, ll], axis=0), hi_ref[0:n, :], 1, 0)
        X = top[0:128] + (top[128:256] + bdot(lh, lo_ref[0:n, :], 1, 0))
        buf[0, 64 * k : 64 * k + 64, :] = X[0:64]
        buf[1, 64 * k : 64 * k + 64, :] = X[64:128]
        if k == 0:
            pl.semaphore_wait(bar, len(targets))
        post(k)
        if k >= 2:
            turn_x(k - 2)
        if k < 3:
            L21 = dot(a_ref[n:, o:n], LI, 1, 1)
            l_ref[n:, o:n] = L21
            a_ref[n:, n:] = a_ref[n:, n:] - dot(L21, L21, 1, 1)
    turn_x(2)
    pl.when(x == 0)(turn_y)
    turn_x(3)
    pl.when(x != 0)(turn_y)
    for h in range(2):
        for d in range(4):
            for e in range(4):
                if d:
                    first(h, d, e).wait_send()
                last(h, d, e, 1).wait()
                if e:
                    last(h, d, e, 0).wait()
            stay(h, d, 0).wait()


def local(tensor):
    f32, bf16, shape = jnp.float32, jnp.bfloat16, jax.ShapeDtypeStruct
    hops = [
        pltpu.SemaphoreType.DMA(n)
        for n in ((2, 4, 4), (2, 4, 4), (2, 4, 4, 2), (2, 4, 4, 2), (2, 4))
    ]
    vmem, dma = pl.BlockSpec(memory_space=pltpu.VMEM), pltpu.SemaphoreType.DMA
    hi, lo, gram = pl.pallas_call(
        gather_gram,
        out_shape=(shape((M, W), bf16), shape((M, W), bf16), shape((PACK, 128), f32)),
        in_specs=[pl.BlockSpec(memory_space=pl.ANY)],
        out_specs=(vmem, vmem, vmem),
        scratch_shapes=[
            pltpu.VMEM((M, W), f32),
            pltpu.VMEM((2, 3, 4, 8, 2 * W), f32),
            pltpu.VMEM((PACK, 128), f32),
            pltpu.VMEM((HALF, 128), f32),
            pltpu.VMEM((HALF, 128), f32),
            pltpu.VMEM((NF // 2, OWN, 128), f32),
            pltpu.VMEM((OWN, 128), f32),
            pltpu.VMEM((NG, OWN, 128), f32),
            *hops,
            dma((2,)),
            dma((2,)),
            dma((30,)),
            dma((30,)),
            dma((14,)),
            dma((14,)),
            dma((30,)),
            dma((30,)),
            dma((32,)),
            dma((32,)),
        ],
        compiler_params=pltpu.CompilerParams(collective_id=0, has_side_effects=True, vmem_limit_bytes=32 << 20),
    )(tensor)
    factor, basis = pl.pallas_call(
        factor_solve_scatter,
        out_shape=(shape((M, M), f32), shape(tensor.shape, f32)),
        in_specs=[vmem] * 3,
        out_specs=(vmem, pl.BlockSpec(memory_space=pl.ANY)),
        scratch_shapes=[
            pltpu.VMEM((M, M), f32),
            pltpu.VMEM((M, M), f32),
            pltpu.VMEM((144, 128), f32),
            pltpu.VMEM((2, M // 2, W), f32),
            pltpu.VMEM((2, 4, 4, 16, W), f32),
            *hops,
        ],
        compiler_params=pltpu.CompilerParams(collective_id=1, has_side_effects=True, vmem_limit_bytes=32 << 20),
    )(gram, hi, lo)
    return basis, factor


def solution(mesh):
    return jax.shard_map(
        local,
        mesh=mesh,
        in_specs=(P("fibre", "group"),),
        out_specs=(P("fibre", "group"), P()),
        check_vma=False,
    )
```

```python
import jax
import jax.numpy as jnp
from jax import lax
from jax.experimental import pallas as pl
from jax.experimental.pallas import tpu as pltpu
from jax.sharding import PartitionSpec as P

HI = lax.Precision.HIGHEST
MESH = pl.DeviceIdType.MESH
M = 512
NF = 32
NG = 8
W = 1536
COLS = W * NF * NG
PACK = 1280
OWN = PACK // NF
HALF = PACK // 2
CHUNKS = ((0, 24), (24, 16))
CHIPS = sorted(
    [(dx, dy) for dx in range(4) for dy in range(4) if (dx, dy) != (0, 0)],
    key=lambda t: -(min(t[0], 4 - t[0]) + min(t[1], 4 - t[1])),
)
FAR = sorted(
    [(dx, dy, dc) for dx in range(4) for dy in range(4) for dc in range(2) if (dx, dy, dc) != (0, 0, 0)],
    key=lambda t: -(min(t[0], 4 - t[0]) + min(t[1], 4 - t[1])),
)


def peer(me, t):
    x, y, c = me // 8, (me // 2) % 4, me % 2
    return ((x + t[0]) % 4 * 4 + (y + t[1]) % 4) * 2 + (c + t[2]) % 2


def chip(x, y, c):
    return ((x % 4) * 4 + y % 4) * 2 + c % 2


def exchange(pair, one, slot, slot_one, dst, sems, local_sem, order=(2, 1, 3), hook=None):
    s1, r1, s2, r2 = sems
    me, g = lax.axis_index("fibre"), lax.axis_index("group")
    x, y, c = me // 8, (me // 2) % 4, me % 2
    first, last, own = {}, [], []

    def go(h, d, e, dc, src, f):
        to = chip(x, y + e, c + dc) if h == 0 else chip(x + e, y, c + dc)
        if e == 0 and dc == 0:
            k = pltpu.make_async_copy(src, dst(h, f), local_sem.at[h, d])
            own.append(k)
        else:
            k = pltpu.make_async_remote_copy(
                src_ref=src, dst_ref=dst(h, f), send_sem=s2.at[h, d, e, dc], recv_sem=r2.at[h, d, e, dc],
                device_id=(to, g), device_id_type=MESH,
            )
            last.append(k)
        k.start()

    for h, d, e in (
        [(h, d, e) for d in order for e in (2, 1, 3, 0) for h in range(2)]
        if hook is None
        else [(h, d, e) for h in range(2) for d in order for e in (2, 1, 3, 0)]
    ):
                if hook is not None and (d, e) == (order[0], 2):
                    hook(h)
                X, Y = (x + d, y + e) if h == 0 else (x + e, y + d)
                to = chip(x + d, y, c) if h == 0 else chip(x, y + d, c)
                k = pltpu.make_async_remote_copy(
                    src_ref=pair(h, X % 4, Y % 4), dst_ref=slot(h, d, e), send_sem=s1.at[h, d, e],
                    recv_sem=r1.at[h, d, e], device_id=(to, g), device_id_type=MESH,
                )
                k.start()
                first[h, d, e] = k
    for e in (2, 1, 3, 0):
        for dc in range(2):
            for h in range(2):
                X, Y = (x, y + e) if h == 0 else (x + e, y)
                go(h, 0, e, dc, one(h, X % 4, Y % 4, (c + dc) % 2), me)
    for d in order:
        for e in (2, 1, 3, 0):
            for h in range(2):
                first[h, d, e].wait_recv()
                f = chip(x - d + 4, y, c) if h == 0 else chip(x, y - d + 4, c)
                for dc in range(2):
                    go(h, d, e, dc, slot_one(h, d, e, (c + dc) % 2), f)
    for k in first.values():
        k.wait_send()
    for k in last + own:
        k.wait()


def cross(me):
    x, y, c = me // 8, (me // 2) % 4, me % 2
    t = [(0, 0, 1)] + [(d, 0, k) for d in (1, 2, 3) for k in (0, 1)] + [(0, d, k) for d in (1, 2, 3) for k in (0, 1)]
    return [chip(x + a, y + b, c + k) for a, b, k in t]


def rows(i, n):
    return pl.ds(pl.multiple_of(i * n, 8), n)


def lanes(i, n):
    return pl.ds(pl.multiple_of(i * n, 128), n)


def bdot(a, b, ca, cb):
    return lax.dot_general(a, b, (((ca,), (cb,)), ((), ())), preferred_element_type=jnp.float32)


def gather_gram(x_ref, hi_ref, lo_ref, g_ref, cols, relay, part, pair, keep, parts, mine, planes, sa, ra, sb, rb, ls,
                s0, r0, s1, r1, s2, r2, s3, r3, s4, r4):
    me, g = lax.axis_index("fibre"), lax.axis_index("group")
    bar = pltpu.get_barrier_semaphore()
    for t in FAR:
        pl.semaphore_signal(bar, inc=1, device_id=(peer(me, t), g), device_id_type=MESH)
    for k in range(1, NG):
        pl.semaphore_signal(bar, inc=1, device_id=(me, (g + k) % NG), device_id_type=MESH)
    pl.semaphore_wait(bar, NF + NG - 2)

    def send(src, dst, to, s, r, i):
        c = pltpu.make_async_remote_copy(
            src_ref=src, dst_ref=dst, send_sem=s.at[i], recv_sem=r.at[i], device_id=to, device_id_type=MESH
        )
        c.start()
        return c

    exchange(
        lambda h, X, Y: x_ref.at[8 * h : 8 * h + 8, lanes(X * 4 + Y, 2 * W)],
        lambda h, X, Y, C: x_ref.at[8 * h : 8 * h + 8, lanes((X * 4 + Y) * 2 + C, W)],
        lambda h, d, e: relay.at[h, d - 1, e],
        lambda h, d, e, C: relay.at[h, d - 1, e, :, lanes(C, W)],
        lambda h, f: cols.at[rows(2 * f + h, 8), :],
        (sa, ra, sb, rb),
        ls,
    )

    for k in range(4):
        v = cols[128 * k : 128 * k + 128, :]
        top = v.astype(jnp.bfloat16)
        hi_ref[128 * k : 128 * k + 128, :] = top
        lo_ref[128 * k : 128 * k + 128, :] = (v - top.astype(jnp.float32)).astype(jnp.bfloat16)
    for i in range(2):
        n = 256 * (i + 1)
        a = hi_ref[n - 256 : n, :]
        both = jnp.concatenate([a, lo_ref[n - 256 : n, :]], axis=0)
        top = bdot(both, hi_ref[0:n, :], 1, 1)
        blk = (top[0:256] + (top[256:512] + bdot(a, lo_ref[0:n, :], 1, 1))) * (1.0 / COLS)
        for r in range(2):
            for j in range(2 * i + r + 1):
                o = 128 * ((2 * i + r) * (2 * i + r + 1) // 2 + j)
                part[o : o + 128, :] = blk[128 * r : 128 * r + 128, 128 * j : 128 * j + 128]

    x, y, c = me // 8, (me // 2) % 4, me % 2
    p, twin = me // 2, (chip(x, y, c + 1), g)
    ks = range(len(CHUNKS))

    def span(core, k):
        return pl.ds(pl.multiple_of(core * HALF + 16 * CHUNKS[k][0], 8), 16 * CHUNKS[k][1])

    def piece(core, k, q):
        return pl.ds(pl.multiple_of(core * HALF + 16 * CHUNKS[k][0] + q * CHUNKS[k][1], 8), CHUNKS[k][1])

    def near(k):
        return pl.ds(16 * CHUNKS[k][0], 16 * CHUNKS[k][1])

    swap = [send(part.at[span(1 - c, k), :], pair.at[near(k), :], twin, s0, r0, k) for k in ks]
    plane = []
    for k in ks:
        swap[k].wait_recv()
        keep[near(k), :] = part[span(c, k), :] + pair[near(k), :]
        o, n = CHUNKS[k]
        cs = []
        for i, t in enumerate(CHIPS):
            q = chip(x + t[0], y + t[1], c)
            src = keep.at[pl.ds(pl.multiple_of(16 * o + (q // 2) * n, 8), n), :]
            cs.append(send(src, parts.at[p, o : o + n, :], (q, g), s1, r1, 15 * k + i))
        parts[p, o : o + n, :] = keep[pl.ds(pl.multiple_of(16 * o + p * n, 8), n), :]
        plane.append(cs)

    def added(ref, count, o, n):
        v = [ref[f, o : o + n, :] for f in range(count)]
        while len(v) > 1:
            v = [v[f] + v[f + 1] for f in range(0, len(v), 2)]
        return v[0]

    depth = []
    for k in ks:
        o, n = CHUNKS[k]
        for q in plane[k]:
            q.wait_recv()
        mine[o : o + n, :] = added(parts, NF // 2, o, n)
        depth.append([
            send(mine.at[o : o + n, :], planes.at[g, o : o + n, :], (me, (g + d) % NG), s2, r2, 7 * k + d - 1)
            for d in (4, 3, 5, 2, 6, 1, 7)
        ])
        planes[g, o : o + n, :] = mine[o : o + n, :]

    spread, over = [], []
    for k in ks:
        o, n = CHUNKS[k]
        for q in depth[k]:
            q.wait_recv()
        g_ref[piece(c, k, p), :] = added(planes, NG, o, n)
        own = g_ref.at[piece(c, k, p), :]
        spread.append([
            send(own, own, (chip(x + t[0], y + t[1], c), g), s3, r3, 15 * k + i) for i, t in enumerate(CHIPS)
        ])
        over.append(send(own, own, twin, s4, r4, 16 * k + 15))
    for k in ks:
        for i in reversed(range(15)):
            t = CHIPS[i]
            spread[k][i].wait_recv()
            got = g_ref.at[piece(c, k, chip(x - t[0] + 4, y - t[1] + 4, 0) // 2), :]
            over.append(send(got, got, twin, s4, r4, 16 * k + i))
    for q in swap + [q for l in plane + depth + spread for q in l]:
        q.wait_send()
    for q in over:
        q.wait()


def dot(a,b,ca=1,cb=0):
    return lax.dot_general(a,b,(((ca,),(cb,)),((),())),precision=HI,preferred_element_type=jnp.float32)
def diag_block(w):
    lane=lax.broadcasted_iota(jnp.int32,(8,128),1)
    sub=lax.broadcasted_iota(jnp.int32,(8,128),0)
    spread=lambda v,r:jnp.broadcast_to(v[r:r+1,:],(8,128))
    def gather(v,base,r):
        return jnp.take_along_axis(v,jnp.full((8,128),jnp.clip(base+r,0,127),jnp.int32),axis=1)
    def total(t):
        return ((t[0]+t[1])+(t[2]+t[3]))+((t[4]+t[5])+(t[6]+t[7]))
    def apply(A,C,W,base):
        group=(lane>=base)&(lane<base+8)
        return jnp.where(group,0.0,A)-total([C[r]*W[r] for r in range(8)])
    rowf=lax.broadcasted_iota(jnp.int32,(128,128),0)
    def make(lo):
      def step(p,carry):
        R,Q,Wp=carry
        base=pl.multiple_of(8*p,8)
        prev=base-8
        B=[gather(R,base,c) for c in range(8)]
        C=[gather(Q,base,r) for r in range(8)]
        S=w[pl.ds(base+16,8),:]
        G1=[gather(S,prev,r) for r in range(8)]
        Wl=[spread(Wp,r) for r in range(8)]
        S=apply(S,G1,Wl,prev)
        G2=[gather(S,base,r) for r in range(8)]
        A=w[8*lo:128,:]
        rowi=lax.broadcasted_iota(jnp.int32,A.shape,0)+8*lo
        lan=lax.broadcasted_iota(jnp.int32,A.shape,1)
        full=jnp.where((rowf>=prev)&(rowf<base),jnp.concatenate([Wp]*16,axis=0),0.0)
        N=jnp.where((lan>=prev)&(lan<base),0.0,A)-dot(A,full)
        w[8*lo:128,:]=jnp.where(rowi>=8*p+24,N,A)
        kept=R
        for r in range(8):
            here=sub==r
            row=spread(R,r)
            kept=jnp.where(here,row,kept)
            inv=1.0/spread(B[r],r)
            m=B[r]*inv
            for c in range(r+1,8):
                rc=spread(B[c],r)
                B[c]=jnp.where(here,rc*inv,B[c]-m*rc)
            hit=lane==base+r
            row=jnp.where(hit,1.0,row)
            R=jnp.where(here,row*inv,jnp.where(hit,0.0,R)-m*row)
        W=[spread(R,r) for r in range(8)]
        newR=apply(Q,C,W,base)
        newQ=apply(S,G2,W,base)
        w[pl.ds(base,8),:]=kept
        return newR,newQ,R
      return step
    carry=(w[0:8,:],w[8:16,:],jnp.zeros((8,128),jnp.float32))
    carry=lax.fori_loop(0,8,make(3),carry)
    lax.fori_loop(8,16,make(11),carry)
def factor_solve_scatter(
    g_ref, hi_ref, lo_ref, l_ref, o_ref, a_ref, li_ref, w, buf, relay, sa, ra, sb, rb, ls
):
    me, g = lax.axis_index("fibre"), lax.axis_index("group")
    x, y, c = me // 8, (me // 2) % 4, me % 2
    bar = pltpu.get_barrier_semaphore()
    targets = cross(me)
    for t in targets:
        pl.semaphore_signal(bar, inc=1, device_id=(t, g), device_id_type=MESH)

    def first(h, d, e):
        X, Y = (x + d, y + e) if h == 0 else (x + e, y + d)
        to = chip(x + d, y, c) if h == 0 else chip(x, y + d, c)
        return pltpu.make_async_remote_copy(
            src_ref=buf.at[h, rows((X % 4) * 4 + Y % 4, 16), :],
            dst_ref=relay.at[h, d, e],
            send_sem=sa.at[h, d, e],
            recv_sem=ra.at[h, d, e],
            device_id=(to, g),
            device_id_type=MESH,
        )

    def place(h, d, e, dc):
        X, Y = (x, y + e) if h == 0 else (x + e, y)
        C = (c + dc) % 2
        if d == 0:
            src, f = buf.at[h, rows(((X % 4) * 4 + Y % 4) * 2 + C, 8), :], me
        else:
            src = relay.at[h, d, e, rows(C, 8), :]
            f = chip(x - d + 4, y, c) if h == 0 else chip(x, y - d + 4, c)
        return src, o_ref.at[8 * h : 8 * h + 8, lanes(f, W)], (chip(X, Y, C), g)

    def last(h, d, e, dc):
        src, dst, to = place(h, d, e, dc)
        return pltpu.make_async_remote_copy(
            src_ref=src, dst_ref=dst, send_sem=sb.at[h, d, e, dc], recv_sem=rb.at[h, d, e, dc],
            device_id=to, device_id_type=MESH,
        )

    def stay(h, d, e):
        src, dst, to = place(h, d, e, 0)
        return pltpu.make_async_copy(src, dst, ls.at[h, d])

    def go(h, d, e):
        last(h, d, e, 1).start()
        if h == 0:
            if e == 0:
                stay(h, d, e).start()
            else:
                last(h, d, e, 0).start()
        else:
            pl.when(e == 0)(lambda: stay(h, d, e).start())
            pl.when(e != 0)(lambda: last(h, d, e, 0).start())

    def post(k):
        off = (k - x + 4) % 4

        @pl.when(off != 0)
        def _():
            for e in (2, 1, 3, 0):
                first(0, off, e).start()

        @pl.when(off == 0)
        def _():
            for e in (2, 1, 3, 0):
                go(0, 0, e)

        for d in (2, 1, 3):
            first(1, d, off).start()
        go(1, 0, off)

    def turn_x(k):
        off = (k - x + 4) % 4
        for d in (2, 1, 3):
            first(1, d, off).wait_recv()
            go(1, d, off)

    def turn_y():
        for d in (2, 1, 3):
            for e in (2, 1, 3, 0):
                first(0, d, e).wait_recv()
                go(0, d, e)

    l_ref[...] = jnp.zeros((M, M), jnp.float32)
    li_ref[...] = jnp.zeros((M, M), jnp.float32)
    B = 128
    for i in range(4):
        for j in range(i + 1):
            b = i * (i + 1) // 2 + j
            a_ref[B * i : B * i + B, B * j : B * j + B] = g_ref[B * b : B * b + B, :]
    ri = lax.broadcasted_iota(jnp.int32, (B, B), 0)
    ci = lax.broadcasted_iota(jnp.int32, (B, B), 1)
    for k in range(4):
        o, n = k * B, (k + 1) * B
        w[0:B, :] = a_ref[o:n, o:n]
        diag_block(w)
        A = w[0:B, :]
        rs = lax.rsqrt(jnp.sum(jnp.where(ri == ci, A, 0.0), axis=1, keepdims=True))
        U = jnp.where(ci >= ri, A, 0.0) * rs
        LI = jnp.where(ci < ri, A, jnp.where(ri == ci, 1.0, 0.0)) * rs
        l_ref[o:n, o:n] = U.T
        if k:
            li_ref[o:n, 0:o] = -dot(LI, dot(l_ref[o:n, 0:o], li_ref[0:o, 0:o]))
        li_ref[o:n, o:n] = LI
        li = li_ref[o:n, 0:n].reshape(8, 2, 8, n)
        li = jnp.concatenate([li[:, 0].reshape(64, n), li[:, 1].reshape(64, n)], axis=0)
        lh = li.astype(jnp.bfloat16)
        ll = (li - lh.astype(jnp.float32)).astype(jnp.bfloat16)
        top = bdot(jnp.concatenate([lh, ll], axis=0), hi_ref[0:n, :], 1, 0)
        X = top[0:128] + (top[128:256] + bdot(lh, lo_ref[0:n, :], 1, 0))
        buf[0, 64 * k : 64 * k + 64, :] = X[0:64]
        buf[1, 64 * k : 64 * k + 64, :] = X[64:128]
        if k == 0:
            pl.semaphore_wait(bar, len(targets))
        post(k)
        if k >= 2:
            turn_x(k - 2)
        if k < 3:
            L21 = dot(a_ref[n:, o:n], LI, 1, 1)
            l_ref[n:, o:n] = L21
            a_ref[n:, n:] = a_ref[n:, n:] - dot(L21, L21, 1, 1)
    turn_x(2)
    pl.when(x == 0)(turn_y)
    turn_x(3)
    pl.when(x != 0)(turn_y)
    for h in range(2):
        for d in range(4):
            for e in range(4):
                if d:
                    first(h, d, e).wait_send()
                last(h, d, e, 1).wait()
                if e:
                    last(h, d, e, 0).wait()
            stay(h, d, 0).wait()


def local(tensor):
    f32, bf16, shape = jnp.float32, jnp.bfloat16, jax.ShapeDtypeStruct
    hops = [
        pltpu.SemaphoreType.DMA(n)
        for n in ((2, 4, 4), (2, 4, 4), (2, 4, 4, 2), (2, 4, 4, 2), (2, 4))
    ]
    vmem, dma = pl.BlockSpec(memory_space=pltpu.VMEM), pltpu.SemaphoreType.DMA
    hi, lo, gram = pl.pallas_call(
        gather_gram,
        out_shape=(shape((M, W), bf16), shape((M, W), bf16), shape((PACK, 128), f32)),
        in_specs=[pl.BlockSpec(memory_space=pltpu.HBM)],
        out_specs=(vmem, vmem, vmem),
        scratch_shapes=[
            pltpu.VMEM((M, W), f32),
            pltpu.VMEM((2, 3, 4, 8, 2 * W), f32),
            pltpu.VMEM((PACK, 128), f32),
            pltpu.VMEM((HALF, 128), f32),
            pltpu.VMEM((HALF, 128), f32),
            pltpu.VMEM((NF // 2, OWN, 128), f32),
            pltpu.VMEM((OWN, 128), f32),
            pltpu.VMEM((NG, OWN, 128), f32),
            *hops,
            dma((2,)),
            dma((2,)),
            dma((30,)),
            dma((30,)),
            dma((14,)),
            dma((14,)),
            dma((30,)),
            dma((30,)),
            dma((32,)),
            dma((32,)),
        ],
        compiler_params=pltpu.CompilerParams(collective_id=0, has_side_effects=True, vmem_limit_bytes=32 << 20),
    )(pltpu.with_memory_space_constraint(tensor, pltpu.HBM))
    factor, basis = pl.pallas_call(
        factor_solve_scatter,
        out_shape=(shape((M, M), f32), shape(tensor.shape, f32)),
        in_specs=[vmem] * 3,
        out_specs=(vmem, pl.BlockSpec(memory_space=pl.ANY)),
        scratch_shapes=[
            pltpu.VMEM((M, M), f32),
            pltpu.VMEM((M, M), f32),
            pltpu.VMEM((144, 128), f32),
            pltpu.VMEM((2, M // 2, W), f32),
            pltpu.VMEM((2, 4, 4, 16, W), f32),
            *hops,
        ],
        compiler_params=pltpu.CompilerParams(collective_id=1, has_side_effects=True, vmem_limit_bytes=32 << 20),
    )(gram, hi, lo)
    return basis, factor


def solution(mesh):
    return jax.shard_map(
        local,
        mesh=mesh,
        in_specs=(P("fibre", "group"),),
        out_specs=(P("fibre", "group"), P()),
        check_vma=False,
    )
```
